768 devices in a mesh: grid: 48 (over y, z_hi, core), band: 16 (over x, z_lo).
Axes of the slice: x: 4, y: 8, z: 12 (z_hi: 3, z_lo: 4; z = z_hi * 4 + z_lo), core: 2. Of those that a mesh axis runs over, the one named last changes fastest.
Arguments:
- orbitals: float32 [1024, 96, 8, 128], P('band', 'grid'), may hold values from -6 to 6
- potential: float32 [96, 8, 128], P('grid'), may hold values from -8 to 8
- rotation: float32 [1024, 1024], P(None, 'band'), may hold values from -0.1875 to 0.1875
Outputs:
- rotated: float32 [1024, 96, 8, 128], P('band', 'grid')
The draws below stay inside these ranges and needn't reach their ends.
All inputs are finite; a program needn't handle non-finite values.
Results may differ from the reference program's by a relative error of at most 0.00007.
Values sent between devices are 32-bit elements; how exact they have to be, the bound alone decides.
No kernel may reach another device: no remote copies, remote signals or barrier semaphores. Data moves between devices by JAX's collectives and lax.ppermute only.
A program may use at most 32 MiB of HBM per device.

```python
import jax
import jax.numpy as jnp
from jax import lax

ORB_DEV = 64
NY = 8
NZ = 128
NB = 1024
NX = 96


def levels(stream_key, extent, shards, least, high):
    factor_of = 1.0
    for axis_at, parts in shards:
        heights = jax.random.uniform(jax.random.fold_in(jax.random.fold_in(stream_key, 6), axis_at), (parts,), jnp.float32, least / len(shards), high / len(shards))
        factor_of = factor_of * jnp.repeat(jnp.exp(heights), extent[axis_at] // parts).reshape((-1,) + (1,) * (len(extent) - 1 - axis_at))
    return factor_of


def normal_values(key, shape, width, bound, cuts=(), held_as=jnp.bfloat16):
    array = jax.random.normal(key, shape, jnp.float32) * width
    if len(cuts) > 0:
        array = levels(key, shape, cuts, -0.22, 0.18) * array
    return jnp.clip(array, min=-bound, max=bound).astype(held_as)


def setup_inputs(seed: int = 0) -> dict:
    key_of = jax.random.split(jax.random.key(seed), 4)
    return {
        "orbitals": normal_values(key_of[0], (NB, NX, NY, NZ), 1.0, 6.0, ((0, 16), (1, 48)), jnp.float32),
        "potential": jnp.clip(jax.random.uniform(key_of[1], (NX, NY, NZ), jnp.float32, -8.0, 8.0) * levels(key_of[1], (NX, NY, NZ), ((0, 48),), -0.4, 0.0), -8.0, 8.0),
        "rotation": normal_values(key_of[2], (NB, NB), NB ** -0.5, 0.1875, ((1, 16),), jnp.float32),
    }


center_shift = 18.0
half_width = 16.0
spacing_square = 0.25


def second_along(states, which_axis):
    nearer = jnp.roll(states, 1, which_axis) + jnp.roll(states, -1, which_axis)
    farther = jnp.roll(states, 2, which_axis) + jnp.roll(states, -2, which_axis)
    return (16.0 * nearer - farther - 30.0 * states) / (12.0 * spacing_square)


def scaled_apply(states, potential):
    laplace = second_along(states, 1) + second_along(states, 2) + second_along(states, 3)
    hamilton = -0.5 * laplace + potential[None] * states
    return (hamilton - center_shift * states) / half_width


def filter_block(states, potential):
    scaled_once = scaled_apply(states, potential)
    return 2.0 * scaled_apply(scaled_once, potential) - states


def reference(orbitals, potential, rotation):
    blocks = orbitals.reshape(-1, ORB_DEV, NX, NY, NZ)

    def filter_one(block):
        return filter_block(block, potential)

    filtered = lax.map(filter_one, blocks)
    filtered = filtered.reshape(NB, NX * NY * NZ)
    rotated = jnp.dot(rotation.T, filtered, precision=lax.Precision.HIGHEST, preferred_element_type=jnp.float32)
    return rotated.reshape(NB, NX, NY, NZ)
```

```python
import jax
import jax.numpy as jnp
from jax import lax
from jax.experimental import pallas as pl
from jax.experimental.pallas import tpu as pltpu
from jax.sharding import PartitionSpec as P

GROUP = 8


def shifted_sums(c, axis):
    n = c.shape[axis]
    near = pltpu.roll(c, 1, axis) + pltpu.roll(c, n - 1, axis)
    far = pltpu.roll(c, 2, axis) + pltpu.roll(c, n - 2, axis)
    return near, far


def apply_plane(c, near_x, far_x, pot):
    near_y, far_y = shifted_sums(c, 1)
    near_z, far_z = shifted_sums(c, 2)
    near = near_x + near_y + near_z
    far = far_x + far_y + far_z
    return c * pot - (1.0 / 6.0) * near + (1.0 / 96.0) * far


def stencil_kernel(combine, par_ref, own, outer, inner, pot_ref, *rest):
    base, out = rest if combine else (None, rest[0])
    par = par_ref[0]
    other = 1 - par
    pot_a = ((pot_ref[par] - 3.0) * 0.0625)[None]
    pot_b = ((pot_ref[other] - 3.0) * 0.0625)[None]

    @pl.loop(0, own.shape[0] // GROUP)
    def _(step):
        rows = pl.ds(step * GROUP, GROUP)
        a, b = own[rows, par], own[rows, other]
        o1, o2 = outer[rows, other], outer[rows, par]
        i1, i2 = inner[rows, par], inner[rows, other]
        sa = apply_plane(a, o1 + b, o2 + i1, pot_a)
        sb = apply_plane(b, a + i1, o1 + i2, pot_b)
        if combine:
            sa = 2.0 * sa - base[rows, par]
            sb = 2.0 * sb - base[rows, other]
        out[rows, par] = sa
        out[rows, other] = sb


def stencil(par, own, outer, inner, pot, base=None):
    combine = base is not None
    args = (own, outer, inner, pot) + ((base,) if combine else ())
    return pl.pallas_call(
        lambda *refs: stencil_kernel(combine, *refs),
        out_shape=jax.ShapeDtypeStruct(own.shape, own.dtype),
        in_specs=[pl.BlockSpec(memory_space=pltpu.SMEM)]
        + [pl.BlockSpec(memory_space=pltpu.VMEM)] * len(args),
        out_specs=pl.BlockSpec(memory_space=pltpu.VMEM),
        name="stencil",
    )(par, *args)


def swap(value, pairs):
    return lax.ppermute(value, "grid", pairs)


def per_device(orbitals, potential, rotation):
    devices = lax.axis_size("grid")
    outer_pairs = [(i, (i + 1 if i % 2 else i - 1) % devices) for i in range(devices)]
    inner_pairs = [(i, i ^ 1) for i in range(devices)]
    par = (lax.axis_index("grid") % 2).astype(jnp.int32).reshape(1)
    rot_t = lax.all_gather(rotation.T, "band", axis=0, tiled=True)

    first = stencil(
        par, orbitals, swap(orbitals, outer_pairs), swap(orbitals, inner_pairs), potential
    )
    filtered = stencil(
        par, first, swap(first, outer_pairs), swap(first, inner_pairs), potential, orbitals
    )
    orbs, planes, ny, nz = orbitals.shape
    groups = lax.axis_size("band")
    rows = planes * ny
    parts = filtered.reshape(orbs, rows, nz).transpose(1, 0, 2)
    parts = lax.all_to_all(parts, "band", 0, 0, tiled=True)
    mixed = jnp.dot(
        rot_t,
        parts.reshape(groups * orbs, nz),
        precision=lax.Precision.HIGH,
        preferred_element_type=jnp.float32,
    )
    back = lax.all_to_all(mixed.reshape(groups, orbs, nz), "band", 0, 0, tiled=True)
    return back.transpose(1, 0, 2).reshape(orbs, planes, ny, nz)


def solution(mesh):
    in_specs = (P("band", "grid", None, None), P("grid", None, None), P(None, "band"))
    out_specs = P("band", "grid", None, None)
    return jax.shard_map(
        per_device, mesh=mesh, in_specs=in_specs, out_specs=out_specs, check_vma=False
    )
```

```python
import jax
import jax.numpy as jnp
import numpy as np
from jax import lax
from jax.experimental import pallas as pl
from jax.experimental.pallas import tpu as pltpu
from jax.sharding import Mesh, PartitionSpec as P

GROUP = 8
GRID = ("y", "zh", "c")
BAND = ("x", "zl")


def shifted_sums(c, axis):
    n = c.shape[axis]
    near = pltpu.roll(c, 1, axis) + pltpu.roll(c, n - 1, axis)
    far = pltpu.roll(c, 2, axis) + pltpu.roll(c, n - 2, axis)
    return near, far


def apply_plane(c, near_x, far_x, pot):
    near_y, far_y = shifted_sums(c, 1)
    near_z, far_z = shifted_sums(c, 2)
    near = near_x + near_y + near_z
    far = far_x + far_y + far_z
    return c * pot - (1.0 / 6.0) * near + (1.0 / 96.0) * far


def stencil_kernel(combine, par_ref, own, outer, inner, pot_ref, *rest):
    base, out = rest if combine else (None, rest[0])
    par = par_ref[0]
    other = 1 - par
    pot_a = ((pot_ref[par] - 3.0) * 0.0625)[None]
    pot_b = ((pot_ref[other] - 3.0) * 0.0625)[None]

    @pl.loop(0, own.shape[0] // GROUP)
    def _(step):
        rows = pl.ds(step * GROUP, GROUP)
        a, b = own[rows, par], own[rows, other]
        o1, o2 = outer[rows, other], outer[rows, par]
        i1, i2 = inner[rows, par], inner[rows, other]
        sa = apply_plane(a, o1 + b, o2 + i1, pot_a)
        sb = apply_plane(b, a + i1, o1 + i2, pot_b)
        if combine:
            sa = 2.0 * sa - base[rows, par]
            sb = 2.0 * sb - base[rows, other]
            out[par, :, rows] = jnp.swapaxes(sa, 0, 1)
            out[other, :, rows] = jnp.swapaxes(sb, 0, 1)
        else:
            out[rows, par] = sa
            out[rows, other] = sb


def in_vmem(value):
    return pltpu.with_memory_space_constraint(value, pltpu.VMEM)


def stencil(par, own, outer, inner, pot, base=None):
    combine = base is not None
    orbs, planes, ny, nz = own.shape
    args = (own, outer, inner, pot) + ((base,) if combine else ())
    shape = (planes, ny, orbs, nz) if combine else own.shape
    return pl.pallas_call(
        lambda *refs: stencil_kernel(combine, *refs),
        out_shape=pltpu.VMEM(shape, own.dtype),
        in_specs=[pl.BlockSpec(memory_space=pltpu.SMEM)]
        + [pl.BlockSpec(memory_space=pltpu.VMEM)] * len(args),
        out_specs=pl.BlockSpec(memory_space=pltpu.VMEM),
        compiler_params=pltpu.CompilerParams(vmem_limit_bytes=4 << 20),
        name="stencil",
    )(par, *map(in_vmem, args))


def rotate_kernel(nx, ny, nzl, at_ref, v, own, own2, near, near2, far, far2, out, wide):
    core, x = at_ref[0], at_ref[1]
    half = own.shape[1]
    value = v[...]
    high = value.astype(jnp.bfloat16)
    low = (value - high.astype(jnp.float32)).astype(jnp.bfloat16)
    wide[...] = jnp.concatenate([high, low], axis=1)
    nz = v.shape[1]

    def product(piece, which):
        high = piece.astype(jnp.bfloat16)
        low = (piece - high.astype(jnp.float32)).astype(jnp.bfloat16)
        rows = pl.ds(pl.multiple_of(which * half, half), half)
        both = jnp.dot(high, wide[rows, :], preferred_element_type=jnp.float32)
        rest = jnp.dot(low, wide[rows, :nz], preferred_element_type=jnp.float32)
        return both[:, :nz] + both[:, nz:] + rest

    def slab(first, second, first_half, slab_x):
        total = product(first, first_half) + product(second, 1 - first_half)
        rows = total.shape[0] // (ny * nzl)
        for y in range(ny):
            for z in range(nzl):
                at = (y * nzl + z) * rows
                out[slab_x * nzl + z, pl.ds(y * rows, rows)] = total[at : at + rows]

    step = 1 - 2 * core
    slab(own[...], own2[...], core, x)
    slab(near[0], near[1], core, lax.rem(x - step + nx, nx))
    slab(near2[0], near2[1], 1 - core, lax.rem(x + step + nx, nx))
    slab(far[...], far2[...], core, lax.rem(x + 2, nx))


def rotate(sizes, at, v, pieces, shape):
    nx, ny, nzl = sizes
    return pl.pallas_call(
        lambda *refs: rotate_kernel(nx, ny, nzl, *refs),
        out_shape=pltpu.VMEM(shape, v.dtype),
        in_specs=[pl.BlockSpec(memory_space=pltpu.SMEM)]
        + [pl.BlockSpec(memory_space=pltpu.VMEM)] * (1 + len(pieces)),
        out_specs=pl.BlockSpec(memory_space=pltpu.VMEM),
        scratch_shapes=[pltpu.VMEM((v.shape[0], 2 * v.shape[1]), jnp.bfloat16)],
        compiler_params=pltpu.CompilerParams(vmem_limit_bytes=24 << 20),
        name="rotate",
    )(at, *map(in_vmem, (v, *pieces)))


def to_all(value, axis):
    copies = jnp.broadcast_to(value[None], (lax.axis_size(axis), *value.shape))
    return lax.all_to_all(copies, axis, 0, 0, tiled=True)


def gather_rotation(rot_t):
    nx, ny = lax.axis_size("x"), lax.axis_size("y")
    rows, cols = rot_t.shape[0] // ny, rot_t.shape[1] // 2
    y, core = lax.axis_index("y"), lax.axis_index("c")
    part = lax.dynamic_slice(rot_t, (y * rows, core * cols), (rows, cols))
    part = to_all(part, "zl")
    own = to_all(part, "y").reshape(-1, cols)
    flip = [(0, 1), (1, 0)]
    line = [(c * nx + i, c * nx + (i + 1 - 2 * c) % nx) for i in range(nx) for c in (0, 1)]
    own2 = lax.ppermute(own, "c", flip)
    near = lax.ppermute(jnp.stack([own, own2]), ("c", "x"), line)
    far = lax.ppermute(near[0], ("c", "x"), line)
    near2 = lax.ppermute(near, "c", flip)
    far2 = lax.ppermute(far, "c", flip)
    return own, own2, near, near2, far, far2


def swap(value, pairs):
    return lax.ppermute(value, GRID, pairs)


def per_device(orbitals, potential, rotation):
    devices = lax.axis_size(GRID)
    outer_pairs = [(i, (i + 1 if i % 2 else i - 1) % devices) for i in range(devices)]
    inner_pairs = [(i, i ^ 1) for i in range(devices)]
    core = lax.axis_index("c").astype(jnp.int32)
    at = jnp.stack([core, lax.axis_index("x").astype(jnp.int32)])
    pieces = gather_rotation(rotation.T)

    outer = swap(orbitals, outer_pairs)
    inner = swap(orbitals, inner_pairs)
    first = stencil(at, orbitals, outer, inner, potential)
    outer = swap(first, outer_pairs)
    inner = swap(first, inner_pairs)
    filtered = stencil(at, first, outer, inner, potential, orbitals)
    orbs, planes, ny, nz = orbitals.shape
    groups = lax.axis_size(BAND)
    parts = filtered.reshape(groups, -1, nz)
    parts = lax.all_to_all(parts, BAND, 0, 0, tiled=True)
    sizes = lax.axis_size("x"), lax.axis_size("y"), lax.axis_size("zl")
    mixed = rotate(sizes, at, parts.reshape(groups * orbs, nz), pieces, (groups, orbs, nz))
    back = lax.all_to_all(mixed, BAND, 0, 0, tiled=True)
    return back.transpose(1, 0, 2).reshape(orbs, planes, ny, nz)


def run(fine):
    in_specs = (P(BAND, GRID, None, None), P(GRID, None, None), P(None, BAND))
    return jax.shard_map(
        per_device, mesh=fine, in_specs=in_specs, out_specs=P(BAND, GRID, None, None), check_vma=False
    )


def solution(mesh):
    devices = np.asarray(mesh.devices).reshape(8, 3, 2, 4, 4)
    fine = Mesh(devices, GRID + BAND)
    return run(fine)
```

```python
import jax
import jax.numpy as jnp
import numpy as np
from jax import lax
from jax.experimental import pallas as pl
from jax.experimental.pallas import tpu as pltpu
from jax.sharding import Mesh, PartitionSpec as P

GROUP = 8
GRID = ("y", "zh", "c")
BAND = ("x", "zl")


def shifted_sums(c, axis):
    n = c.shape[axis]
    near = pltpu.roll(c, 1, axis) + pltpu.roll(c, n - 1, axis)
    far = pltpu.roll(c, 2, axis) + pltpu.roll(c, n - 2, axis)
    return near, far


def apply_plane(c, near_x, far_x, pot):
    near_y, far_y = shifted_sums(c, 1)
    near_z, far_z = shifted_sums(c, 2)
    near = near_x + near_y + near_z
    far = far_x + far_y + far_z
    return c * pot - (1.0 / 6.0) * near + (1.0 / 96.0) * far


def stencil_kernel(combine, par_ref, own, outer, inner, pot_ref, *rest):
    base, out = rest if combine else (None, rest[0])
    par = par_ref[0]
    other = 1 - par
    pot_a = ((pot_ref[par] - 3.0) * 0.0625)[None]
    pot_b = ((pot_ref[other] - 3.0) * 0.0625)[None]

    @pl.loop(0, own.shape[0] // GROUP)
    def _(step):
        rows = pl.ds(step * GROUP, GROUP)
        a, b = own[rows, par], own[rows, other]
        o1, o2 = outer[rows, other], outer[rows, par]
        i1, i2 = inner[rows, par], inner[rows, other]
        sa = apply_plane(a, o1 + b, o2 + i1, pot_a)
        sb = apply_plane(b, a + i1, o1 + i2, pot_b)
        if combine:
            sa = 2.0 * sa - base[rows, par]
            sb = 2.0 * sb - base[rows, other]
            out[par, :, rows] = jnp.swapaxes(sa, 0, 1)
            out[other, :, rows] = jnp.swapaxes(sb, 0, 1)
        else:
            out[rows, par] = sa
            out[rows, other] = sb


def in_vmem(value):
    return pltpu.with_memory_space_constraint(value, pltpu.VMEM)


def stencil(par, own, outer, inner, pot, base=None):
    combine = base is not None
    orbs, planes, ny, nz = own.shape
    args = (own, outer, inner, pot) + ((base,) if combine else ())
    shape = (planes, ny, orbs, nz) if combine else own.shape
    return pl.pallas_call(
        lambda *refs: stencil_kernel(combine, *refs),
        out_shape=pltpu.VMEM(shape, own.dtype),
        in_specs=[pl.BlockSpec(memory_space=pltpu.SMEM)]
        + [pl.BlockSpec(memory_space=pltpu.VMEM)] * len(args),
        out_specs=pl.BlockSpec(memory_space=pltpu.VMEM),
        compiler_params=pltpu.CompilerParams(vmem_limit_bytes=4 << 20),
        name="stencil",
    )(par, *map(in_vmem, args))


def rotate_kernel(nx, at_ref, v, own, own2, near, near2, far, far2, out, wide):
    core, x, odd = at_ref[0], at_ref[1], at_ref[2]
    _, nzl, rows, half = own.shape
    value = v[...]
    high = value.astype(jnp.bfloat16)
    low = (value - high.astype(jnp.float32)).astype(jnp.bfloat16)
    wide[...] = jnp.concatenate([high, low], axis=1)
    nz = v.shape[1]

    def product(piece, which):
        high = piece.astype(jnp.bfloat16)
        low = (piece - high.astype(jnp.float32)).astype(jnp.bfloat16)
        rows = pl.ds(pl.multiple_of(which * half, half), half)
        both = jnp.dot(high, wide[rows, :], preferred_element_type=jnp.float32)
        rest = jnp.dot(low, wide[rows, :nz], preferred_element_type=jnp.float32)
        return both[:, :nz] + both[:, nz:] + rest

    def slab(first, second, first_half, slab_x):
        for pair in (0, 1):
            total = product(first[pair].reshape(nzl * rows, half), first_half)
            total += product(second[pair].reshape(nzl * rows, half), 1 - first_half)
            place = pl.ds(pl.multiple_of((odd ^ pair) * rows, rows), rows)
            for z in range(nzl):
                out[slab_x * nzl + z, place] = total[z * rows : (z + 1) * rows]

    step = 1 - 2 * core
    slab(own, own2, core, x)
    slab(near.at[0], near.at[1], core, lax.rem(x - step + nx, nx))
    slab(near2.at[0], near2.at[1], 1 - core, lax.rem(x + step + nx, nx))
    slab(far, far2, core, lax.rem(x + 2, nx))


def rotate(nx, at, v, pieces, shape):
    return pl.pallas_call(
        lambda *refs: rotate_kernel(nx, *refs),
        out_shape=pltpu.VMEM(shape, v.dtype),
        in_specs=[pl.BlockSpec(memory_space=pltpu.SMEM)]
        + [pl.BlockSpec(memory_space=pltpu.VMEM)] * (1 + len(pieces)),
        out_specs=pl.BlockSpec(memory_space=pltpu.VMEM),
        scratch_shapes=[pltpu.VMEM((v.shape[0], 2 * v.shape[1]), jnp.bfloat16)],
        compiler_params=pltpu.CompilerParams(vmem_limit_bytes=24 << 20),
        name="rotate",
    )(at, *map(in_vmem, (v, *pieces)))


def to_all(value, axis):
    copies = jnp.broadcast_to(value[None], (lax.axis_size(axis), *value.shape))
    return lax.all_to_all(copies, axis, 0, 0, tiled=True)


def gather_rotation(rot_t):
    nx, ny = lax.axis_size("x"), lax.axis_size("y")
    rows, cols = rot_t.shape[0] // 2, rot_t.shape[1] // 2
    y, core = lax.axis_index("y"), lax.axis_index("c")
    part = lax.dynamic_slice(rot_t, ((y % 2) * rows, core * cols), (rows, cols))
    part = to_all(part, "zl")
    pair = lax.ppermute(part, "y", [(i, i ^ 1) for i in range(ny)])
    flip = [(0, 1), (1, 0)]
    line = [(c * nx + i, c * nx + (i + 1 - 2 * c) % nx) for i in range(nx) for c in (0, 1)]
    own = jnp.stack([part, pair])
    own2 = lax.ppermute(own, "c", flip)
    near = lax.ppermute(jnp.stack([own, own2]), ("c", "x"), line)
    far = lax.ppermute(near[0], ("c", "x"), line)
    near2 = lax.ppermute(near, "c", flip)
    far2 = lax.ppermute(far, "c", flip)
    return own, own2, near, near2, far, far2


def swap(value, pairs):
    return lax.ppermute(value, GRID, pairs)


def per_device(orbitals, potential, rotation):
    devices = lax.axis_size(GRID)
    outer_pairs = [(i, (i + 1 if i % 2 else i - 1) % devices) for i in range(devices)]
    inner_pairs = [(i, i ^ 1) for i in range(devices)]
    core = lax.axis_index("c")
    at = jnp.stack([core, lax.axis_index("x"), lax.axis_index("y") % 2]).astype(jnp.int32)
    pieces = gather_rotation(rotation.T)

    outer = swap(orbitals, outer_pairs)
    inner = swap(orbitals, inner_pairs)
    first = stencil(at, orbitals, outer, inner, potential)
    outer = swap(first, outer_pairs)
    inner = swap(first, inner_pairs)
    filtered = stencil(at, first, outer, inner, potential, orbitals)
    orbs, planes, ny, nz = orbitals.shape
    groups = lax.axis_size(BAND)
    parts = filtered.reshape(groups, -1, nz)
    parts = lax.all_to_all(parts, BAND, 0, 0, tiled=True)
    mixed = rotate(lax.axis_size("x"), at, parts.reshape(groups * orbs, nz), pieces, (groups, orbs, nz))
    back = lax.all_to_all(mixed, BAND, 0, 0, tiled=True)
    return back.transpose(1, 0, 2).reshape(orbs, planes, ny, nz)


def run(fine):
    in_specs = (P(BAND, GRID, None, None), P(GRID, None, None), P(None, BAND))
    return jax.shard_map(
        per_device, mesh=fine, in_specs=in_specs, out_specs=P(BAND, GRID, None, None), check_vma=False
    )


def solution(mesh):
    devices = np.asarray(mesh.devices).reshape(8, 3, 2, 4, 4)
    fine = Mesh(devices, GRID + BAND)
    return run(fine)
```

```python
import jax
import jax.numpy as jnp
import numpy as np
from jax import lax
from jax.experimental import pallas as pl
from jax.experimental.pallas import tpu as pltpu
from jax.sharding import Mesh, PartitionSpec as P

GROUP = 8
GRID = ("yh", "yp", "zh", "c")
BAND = ("x", "zl")


def shifted_sums(c, axis):
    n = c.shape[axis]
    near = pltpu.roll(c, 1, axis) + pltpu.roll(c, n - 1, axis)
    far = pltpu.roll(c, 2, axis) + pltpu.roll(c, n - 2, axis)
    return near, far


def apply_plane(c, near_x, far_x, pot):
    near_y, far_y = shifted_sums(c, 1)
    near_z, far_z = shifted_sums(c, 2)
    near = near_x + near_y + near_z
    far = far_x + far_y + far_z
    return c * pot - (1.0 / 6.0) * near + (1.0 / 96.0) * far


def stencil_kernel(combine, par_ref, own, outer, inner, pot_ref, *rest):
    base, out = (rest[0], rest[-1]) if combine else (None, rest[0])
    par = par_ref[0]
    other = 1 - par
    pot_a = ((pot_ref[par] - 3.0) * 0.0625)[None]
    pot_b = ((pot_ref[other] - 3.0) * 0.0625)[None]

    @pl.loop(0, own.shape[0] // GROUP)
    def _(step):
        rows = pl.ds(step * GROUP, GROUP)
        a, b = own[rows, par], own[rows, other]
        o1, o2 = outer[rows, other], outer[rows, par]
        i1, i2 = inner[rows, par], inner[rows, other]
        sa = apply_plane(a, o1 + b, o2 + i1, pot_a)
        sb = apply_plane(b, a + i1, o1 + i2, pot_b)
        if combine:
            sa = 2.0 * sa - base[rows, par]
            sb = 2.0 * sb - base[rows, other]
            out[par, :, rows] = jnp.swapaxes(sa, 0, 1)
            out[other, :, rows] = jnp.swapaxes(sb, 0, 1)
        else:
            out[rows, par] = sa
            out[rows, other] = sb


def in_vmem(value):
    return pltpu.with_memory_space_constraint(value, pltpu.VMEM)


def stencil(par, own, outer, inner, pot, base=None, token=None):
    combine = base is not None
    orbs, planes, ny, nz = own.shape
    args = (own, outer, inner, pot) + ((base, token) if combine else ())
    shape = (planes, ny, orbs, nz) if combine else own.shape
    return pl.pallas_call(
        lambda *refs: stencil_kernel(combine, *refs),
        out_shape=pltpu.VMEM(shape, own.dtype),
        in_specs=[pl.BlockSpec(memory_space=pltpu.SMEM)]
        + [pl.BlockSpec(memory_space=pltpu.VMEM)] * len(args),
        out_specs=pl.BlockSpec(memory_space=pltpu.VMEM),
        compiler_params=pltpu.CompilerParams(vmem_limit_bytes=4 << 20),
        name="stencil",
    )(par, *map(in_vmem, args))


def rotate_kernel(nx, at_ref, v, own, near, near2, far, out, wide):
    core, x = at_ref[0], at_ref[1]
    _, nzl, rows, half = own.shape
    value = v[...]
    high = value.astype(jnp.bfloat16)
    low = (value - high.astype(jnp.float32)).astype(jnp.bfloat16)
    wide[...] = jnp.concatenate([high, low], axis=1)
    nz = v.shape[1]

    def product(piece, which):
        high = piece.astype(jnp.bfloat16)
        low = (piece - high.astype(jnp.float32)).astype(jnp.bfloat16)
        at = which * half
        both = jnp.dot(high, wide[at : at + half, :], preferred_element_type=jnp.float32)
        rest = jnp.dot(low, wide[at : at + half, :nz], preferred_element_type=jnp.float32)
        return both[:, :nz] + both[:, nz:] + rest

    def slab(ref, slab_x):
        for pair in (0, 1):
            total = product(ref[2 * pair].reshape(nzl * rows, half), 0)
            total += product(ref[2 * pair + 1].reshape(nzl * rows, half), 1)
            for z in range(nzl):
                out[slab_x * nzl + z, pair * rows : (pair + 1) * rows] = total[z * rows : (z + 1) * rows]

    step = 1 - 2 * core
    slab(own, x)
    slab(near, lax.rem(x - step + nx, nx))
    slab(near2, lax.rem(x + step + nx, nx))
    slab(far, lax.rem(x + 2, nx))


def rotate(nx, at, v, pieces, shape):
    return pl.pallas_call(
        lambda *refs: rotate_kernel(nx, *refs),
        out_shape=pltpu.VMEM(shape, v.dtype),
        in_specs=[pl.BlockSpec(memory_space=pltpu.SMEM)]
        + [pl.BlockSpec(memory_space=pltpu.VMEM)] * (1 + len(pieces)),
        out_specs=pl.BlockSpec(memory_space=pltpu.VMEM),
        scratch_shapes=[pltpu.VMEM((v.shape[0], 2 * v.shape[1]), jnp.bfloat16)],
        compiler_params=pltpu.CompilerParams(vmem_limit_bytes=24 << 20),
        name="rotate",
    )(at, *map(in_vmem, (v, *pieces)))


def to_all(value, axis):
    copies = jnp.broadcast_to(value[None], (lax.axis_size(axis), *value.shape))
    return lax.all_to_all(copies, axis, 0, 0, tiled=True)


def gather_rotation(rot_t):
    nx = lax.axis_size("x")
    rows, cols = rot_t.shape[0] // 2, rot_t.shape[1] // 2
    at = (lax.axis_index("yp") * rows, lax.axis_index("c") * cols)
    part = to_all(lax.dynamic_slice(rot_t, at, (rows, cols)), "zl")
    own = to_all(part, ("yp", "c"))
    line = [(c * nx + i, c * nx + (i + 1 - 2 * c) % nx) for i in range(nx) for c in (0, 1)]
    near = lax.ppermute(own, ("c", "x"), line)
    far = lax.ppermute(near, ("c", "x"), line)
    near2 = lax.ppermute(near, "c", [(0, 1), (1, 0)])
    token = near[0, 0, :8, :128] * 2.0
    return (own, near, near2, far), token


def swap(value, pairs):
    return lax.ppermute(value, GRID, pairs)


def per_device(orbitals, potential, rotation):
    devices = lax.axis_size(GRID)
    outer_pairs = [(i, (i + 1 if i % 2 else i - 1) % devices) for i in range(devices)]
    inner_pairs = [(i, i ^ 1) for i in range(devices)]
    core = lax.axis_index("c")
    at = jnp.stack([core, lax.axis_index("x")]).astype(jnp.int32)
    pieces, token = gather_rotation(rotation.T)

    outer = swap(orbitals, outer_pairs)
    inner = swap(orbitals, inner_pairs)
    first = stencil(at, orbitals, outer, inner, potential)
    outer = swap(first, outer_pairs)
    inner = swap(first, inner_pairs)
    filtered = stencil(at, first, outer, inner, potential, orbitals, token)
    orbs, planes, ny, nz = orbitals.shape
    groups = lax.axis_size(BAND)
    parts = filtered.reshape(groups, -1, nz)
    parts = lax.all_to_all(parts, BAND, 0, 0, tiled=True)
    mixed = rotate(lax.axis_size("x"), at, parts.reshape(groups * orbs, nz), pieces, (groups, orbs, nz))
    back = lax.all_to_all(mixed, BAND, 0, 0, tiled=True)
    return back.transpose(1, 0, 2).reshape(orbs, planes, ny, nz)


def run(fine):
    in_specs = (P(BAND, GRID, None, None), P(GRID, None, None), P(None, BAND))
    return jax.shard_map(
        per_device, mesh=fine, in_specs=in_specs, out_specs=P(BAND, GRID, None, None), check_vma=False
    )


def solution(mesh):
    devices = np.asarray(mesh.devices).reshape(4, 2, 3, 2, 4, 4)
    fine = Mesh(devices, GRID + BAND)
    return run(fine)
```

```python
import jax
import jax.numpy as jnp
import numpy as np
from jax import lax
from jax.experimental import pallas as pl
from jax.experimental.pallas import tpu as pltpu
from jax.sharding import Mesh, PartitionSpec as P

GROUP = 8
GRID = ("yh", "yp", "zh", "c")
BAND = ("x", "zl")


def shifted_sums(c, axis):
    n = c.shape[axis]
    near = pltpu.roll(c, 1, axis) + pltpu.roll(c, n - 1, axis)
    far = pltpu.roll(c, 2, axis) + pltpu.roll(c, n - 2, axis)
    return near, far


def apply_plane(c, near_x, far_x, pot):
    near_y, far_y = shifted_sums(c, 1)
    near_z, far_z = shifted_sums(c, 2)
    near = near_x + near_y + near_z
    far = far_x + far_y + far_z
    return c * pot - (1.0 / 6.0) * near + (1.0 / 96.0) * far


def stencil_kernel(combine, par_ref, own, outer, inner, pot_ref, *rest):
    base, out = rest if combine else (None, rest[0])
    par = par_ref[0]
    other = 1 - par
    pot_a = ((pot_ref[par] - 3.0) * 0.0625)[None]
    pot_b = ((pot_ref[other] - 3.0) * 0.0625)[None]

    @pl.loop(0, own.shape[0] // GROUP)
    def _(step):
        rows = pl.ds(step * GROUP, GROUP)
        a, b = own[rows, par], own[rows, other]
        o1, o2 = outer[rows, other], outer[rows, par]
        i1, i2 = inner[rows, par], inner[rows, other]
        sa = apply_plane(a, o1 + b, o2 + i1, pot_a)
        sb = apply_plane(b, a + i1, o1 + i2, pot_b)
        if combine:
            sa = 2.0 * sa - base[rows, par]
            sb = 2.0 * sb - base[rows, other]
            out[par, :, rows] = jnp.swapaxes(sa, 0, 1)
            out[other, :, rows] = jnp.swapaxes(sb, 0, 1)
        else:
            out[rows, par] = sa
            out[rows, other] = sb


def in_vmem(value):
    return pltpu.with_memory_space_constraint(value, pltpu.VMEM)


def stencil(par, own, outer, inner, pot, base=None):
    combine = base is not None
    orbs, planes, ny, nz = own.shape
    args = (own, outer, inner, pot) + ((base,) if combine else ())
    shape = (planes, ny, orbs, nz) if combine else own.shape
    return pl.pallas_call(
        lambda *refs: stencil_kernel(combine, *refs),
        out_shape=pltpu.VMEM(shape, own.dtype),
        in_specs=[pl.BlockSpec(memory_space=pltpu.SMEM)]
        + [pl.BlockSpec(memory_space=pltpu.VMEM)] * len(args),
        out_specs=pl.BlockSpec(memory_space=pltpu.VMEM),
        compiler_params=pltpu.CompilerParams(vmem_limit_bytes=4 << 20),
        name="stencil",
    )(par, *map(in_vmem, args))


def rotate_kernel(nx, at_ref, v, own, near, near2, far, out, wide):
    core, x = at_ref[0], at_ref[1]
    _, nzl, rows, half = own.shape
    value = v[...]
    high = value.astype(jnp.bfloat16)
    low = (value - high.astype(jnp.float32)).astype(jnp.bfloat16)
    wide[...] = jnp.concatenate([high, low], axis=1)
    nz = v.shape[1]

    def product(piece, which):
        high = piece.astype(jnp.bfloat16)
        low = (piece - high.astype(jnp.float32)).astype(jnp.bfloat16)
        at = which * half
        both = jnp.dot(high, wide[at : at + half, :], preferred_element_type=jnp.float32)
        rest = jnp.dot(low, wide[at : at + half, :nz], preferred_element_type=jnp.float32)
        return both[:, :nz] + both[:, nz:] + rest

    def slab(ref, slab_x):
        for pair in (0, 1):
            total = product(ref[2 * pair].reshape(nzl * rows, half), 0)
            total += product(ref[2 * pair + 1].reshape(nzl * rows, half), 1)
            for z in range(nzl):
                out[slab_x * nzl + z, pair * rows : (pair + 1) * rows] = total[z * rows : (z + 1) * rows]

    step = 1 - 2 * core
    slab(own, x)
    slab(near, lax.rem(x - step + nx, nx))
    slab(near2, lax.rem(x + step + nx, nx))
    slab(far, lax.rem(x + 2, nx))


def rotate(nx, at, v, pieces, shape):
    return pl.pallas_call(
        lambda *refs: rotate_kernel(nx, *refs),
        out_shape=pltpu.VMEM(shape, v.dtype),
        in_specs=[pl.BlockSpec(memory_space=pltpu.SMEM)]
        + [pl.BlockSpec(memory_space=pltpu.VMEM)] * (1 + len(pieces)),
        out_specs=pl.BlockSpec(memory_space=pltpu.VMEM),
        scratch_shapes=[pltpu.VMEM((v.shape[0], 2 * v.shape[1]), jnp.bfloat16)],
        compiler_params=pltpu.CompilerParams(vmem_limit_bytes=24 << 20),
        name="rotate",
    )(at, *map(in_vmem, (v, *pieces)))


def to_all(value, axis):
    copies = jnp.broadcast_to(value[None], (lax.axis_size(axis), *value.shape))
    return lax.all_to_all(copies, axis, 0, 0, tiled=True)


def gather_rotation(rot_t):
    nx = lax.axis_size("x")
    rows, cols = rot_t.shape[0] // 2, rot_t.shape[1] // 2
    at = (lax.axis_index("yp") * rows, lax.axis_index("c") * cols)
    part = to_all(lax.dynamic_slice(rot_t, at, (rows, cols)), "zl")
    own = to_all(part, ("yp", "c"))
    line = [(c * nx + i, c * nx + (i + 1 - 2 * c) % nx) for i in range(nx) for c in (0, 1)]
    near = lax.ppermute(own, ("c", "x"), line)
    far = lax.ppermute(near, ("c", "x"), line)
    near2 = lax.ppermute(near, "c", [(0, 1), (1, 0)])
    return own, near, near2, far


def swap(value, pairs):
    return lax.ppermute(value, GRID, pairs)


def per_device(orbitals, potential, rotation):
    devices = lax.axis_size(GRID)
    outer_pairs = [(i, (i + 1 if i % 2 else i - 1) % devices) for i in range(devices)]
    inner_pairs = [(i, i ^ 1) for i in range(devices)]
    core = lax.axis_index("c")
    at = jnp.stack([core, lax.axis_index("x")]).astype(jnp.int32)
    pieces = gather_rotation(rotation.T)

    outer = swap(orbitals, outer_pairs)
    inner = swap(orbitals, inner_pairs)
    first = stencil(at, orbitals, outer, inner, potential)
    outer = swap(first, outer_pairs)
    inner = swap(first, inner_pairs)
    filtered = stencil(at, first, outer, inner, potential, orbitals)
    orbs, planes, ny, nz = orbitals.shape
    groups = lax.axis_size(BAND)
    parts = filtered.reshape(groups, -1, nz)
    parts = lax.all_to_all(parts, BAND, 0, 0, tiled=True)
    mixed = rotate(lax.axis_size("x"), at, parts.reshape(groups * orbs, nz), pieces, (groups, orbs, nz))
    back = lax.all_to_all(mixed, BAND, 0, 0, tiled=True)
    return back.transpose(1, 0, 2).reshape(orbs, planes, ny, nz)


def run(fine):
    in_specs = (P(BAND, GRID, None, None), P(GRID, None, None), P(None, BAND))
    return jax.shard_map(
        per_device, mesh=fine, in_specs=in_specs, out_specs=P(BAND, GRID, None, None), check_vma=False
    )


def solution(mesh):
    devices = np.asarray(mesh.devices).reshape(4, 2, 3, 2, 4, 4)
    fine = Mesh(devices, GRID + BAND)
    return run(fine)
```

```python
import jax
import jax.numpy as jnp
import numpy as np
from jax import lax
from jax.experimental import pallas as pl
from jax.experimental.pallas import tpu as pltpu
from jax.sharding import Mesh, PartitionSpec as P

GROUP = 8
GRID = ("y", "zh", "c")
BAND = ("x", "zl")


def shifted_sums(c, axis):
    n = c.shape[axis]
    near = pltpu.roll(c, 1, axis) + pltpu.roll(c, n - 1, axis)
    far = pltpu.roll(c, 2, axis) + pltpu.roll(c, n - 2, axis)
    return near, far


def apply_plane(c, near_x, far_x, pot):
    near_y, far_y = shifted_sums(c, 1)
    near_z, far_z = shifted_sums(c, 2)
    near = near_x + near_y + near_z
    far = far_x + far_y + far_z
    return c * pot - (1.0 / 6.0) * near + (1.0 / 96.0) * far


def stencil_kernel(combine, par_ref, own, outer, inner, pot_ref, *rest):
    base, out = (rest[0], rest[-1]) if combine else (None, rest[0])
    par = par_ref[0]
    other = 1 - par
    pot_a = ((pot_ref[par] - 3.0) * 0.0625)[None]
    pot_b = ((pot_ref[other] - 3.0) * 0.0625)[None]

    @pl.loop(0, own.shape[0] // GROUP)
    def _(step):
        rows = pl.ds(step * GROUP, GROUP)
        a, b = own[rows, par], own[rows, other]
        o1, o2 = outer[rows, other], outer[rows, par]
        i1, i2 = inner[rows, par], inner[rows, other]
        sa = apply_plane(a, o1 + b, o2 + i1, pot_a)
        sb = apply_plane(b, a + i1, o1 + i2, pot_b)
        if combine:
            sa = 2.0 * sa - base[rows, par]
            sb = 2.0 * sb - base[rows, other]
            out[par, :, rows] = jnp.swapaxes(sa, 0, 1)
            out[other, :, rows] = jnp.swapaxes(sb, 0, 1)
        else:
            out[rows, par] = sa
            out[rows, other] = sb


def in_vmem(value):
    return pltpu.with_memory_space_constraint(value, pltpu.VMEM)


def stencil(par, own, outer, inner, pot, base=None):
    combine = base is not None
    orbs, planes, ny, nz = own.shape
    args = (own, outer, inner, pot) + ((base,) if combine else ())
    shape = (planes, ny, orbs, nz) if combine else own.shape
    return pl.pallas_call(
        lambda *refs: stencil_kernel(combine, *refs),
        out_shape=pltpu.VMEM(shape, own.dtype),
        in_specs=[pl.BlockSpec(memory_space=pltpu.SMEM)]
        + [pl.BlockSpec(memory_space=pltpu.VMEM)] * len(args),
        out_specs=pl.BlockSpec(memory_space=pltpu.VMEM),
        compiler_params=pltpu.CompilerParams(vmem_limit_bytes=4 << 20),
        name="stencil",
    )(par, *map(in_vmem, args))


def rotate_kernel(at_ref, v, own, other, out, wide):
    core = at_ref[0]
    ny, nx, nzl, rows, half = own.shape
    value = v[...]
    high = value.astype(jnp.bfloat16)
    low = (value - high.astype(jnp.float32)).astype(jnp.bfloat16)
    wide[...] = jnp.concatenate([high, low], axis=1)
    nz = v.shape[1]

    def product(piece, which):
        piece = piece.reshape(ny * nzl * rows, half)
        high = piece.astype(jnp.bfloat16)
        low = (piece - high.astype(jnp.float32)).astype(jnp.bfloat16)
        at = pl.ds(pl.multiple_of(which * half, half), half)
        both = jnp.dot(high, wide[at, :], preferred_element_type=jnp.float32)
        rest = jnp.dot(low, wide[at, :nz], preferred_element_type=jnp.float32)
        return both[:, :nz] + both[:, nz:] + rest

    for x in range(nx):
        total = product(own[:, x], core) + product(other[:, x], 1 - core)
        for y in range(ny):
            for z in range(nzl):
                at = (y * nzl + z) * rows
                out[x * nzl + z, y * rows : (y + 1) * rows] = total[at : at + rows]


def rotate(at, v, pieces, shape):
    return pl.pallas_call(
        rotate_kernel,
        out_shape=pltpu.VMEM(shape, v.dtype),
        in_specs=[pl.BlockSpec(memory_space=pltpu.SMEM)]
        + [pl.BlockSpec(memory_space=pltpu.VMEM)] * (1 + len(pieces)),
        out_specs=pl.BlockSpec(memory_space=pltpu.VMEM),
        scratch_shapes=[pltpu.VMEM((v.shape[0], 2 * v.shape[1]), jnp.bfloat16)],
        compiler_params=pltpu.CompilerParams(vmem_limit_bytes=24 << 20),
        name="rotate",
    )(at, *map(in_vmem, (v, *pieces)))


def to_all(value, axis):
    copies = jnp.broadcast_to(value[None], (lax.axis_size(axis), *value.shape))
    return lax.all_to_all(copies, axis, 0, 0, tiled=True)


def gather_rotation(rot_t):
    rows, cols = rot_t.shape[0] // lax.axis_size("y"), rot_t.shape[1] // 2
    at = (lax.axis_index("y") * rows, lax.axis_index("c") * cols)
    part = to_all(lax.dynamic_slice(rot_t, at, (rows, cols)), "zl")
    part = to_all(part, "x")
    own = to_all(part, "y")
    other = lax.ppermute(own, "c", [(0, 1), (1, 0)])
    return own, other


def swap(value, pairs):
    return lax.ppermute(value, GRID, pairs)


def per_device(orbitals, potential, rotation):
    devices = lax.axis_size(GRID)
    outer_pairs = [(i, (i + 1 if i % 2 else i - 1) % devices) for i in range(devices)]
    inner_pairs = [(i, i ^ 1) for i in range(devices)]
    core = lax.axis_index("c")
    at = core.astype(jnp.int32).reshape(1)
    pieces = gather_rotation(rotation.T)

    outer = swap(orbitals, outer_pairs)
    inner = swap(orbitals, inner_pairs)
    first = stencil(at, orbitals, outer, inner, potential)
    outer = swap(first, outer_pairs)
    inner = swap(first, inner_pairs)
    filtered = stencil(at, first, outer, inner, potential, orbitals)
    orbs, planes, ny, nz = orbitals.shape
    groups = lax.axis_size(BAND)
    parts = filtered.reshape(groups, -1, nz)
    parts = lax.all_to_all(parts, BAND, 0, 0, tiled=True)
    mixed = rotate(at, parts.reshape(groups * orbs, nz), pieces, (groups, orbs, nz))
    back = lax.all_to_all(mixed, BAND, 0, 0, tiled=True)
    return back.transpose(1, 0, 2).reshape(orbs, planes, ny, nz)


def run(fine):
    in_specs = (P(BAND, GRID, None, None), P(GRID, None, None), P(None, BAND))
    return jax.shard_map(
        per_device, mesh=fine, in_specs=in_specs, out_specs=P(BAND, GRID, None, None), check_vma=False
    )


def solution(mesh):
    devices = np.asarray(mesh.devices).reshape(8, 3, 2, 4, 4)
    fine = Mesh(devices, GRID + BAND)
    return run(fine)
```

```python
import jax
import jax.numpy as jnp
import numpy as np
from jax import lax
from jax.experimental import pallas as pl
from jax.experimental.pallas import tpu as pltpu
from jax.sharding import Mesh, PartitionSpec as P

GROUP = 8
GRID = ("y", "zh", "c")
BAND = ("x", "zl")


def shifted_sums(c, axis):
    n = c.shape[axis]
    near = pltpu.roll(c, 1, axis) + pltpu.roll(c, n - 1, axis)
    far = pltpu.roll(c, 2, axis) + pltpu.roll(c, n - 2, axis)
    return near, far


def apply_plane(c, near_x, far_x, pot):
    near_y, far_y = shifted_sums(c, 1)
    near_z, far_z = shifted_sums(c, 2)
    near = near_x + near_y + near_z
    far = far_x + far_y + far_z
    return c * pot - (1.0 / 6.0) * near + (1.0 / 96.0) * far


def stencil_kernel(combine, par_ref, own, outer, inner, pot_ref, *rest):
    base, out = (rest[0], rest[-1]) if combine else (None, rest[0])
    par = par_ref[0]
    other = 1 - par
    pot_a = ((pot_ref[par] - 3.0) * 0.0625)[None]
    pot_b = ((pot_ref[other] - 3.0) * 0.0625)[None]

    @pl.loop(0, own.shape[0] // GROUP)
    def _(step):
        rows = pl.ds(step * GROUP, GROUP)
        a, b = own[rows, par], own[rows, other]
        o1, o2 = outer[rows, other], outer[rows, par]
        i1, i2 = inner[rows, par], inner[rows, other]
        sa = apply_plane(a, o1 + b, o2 + i1, pot_a)
        sb = apply_plane(b, a + i1, o1 + i2, pot_b)
        if combine:
            sa = 2.0 * sa - base[rows, par]
            sb = 2.0 * sb - base[rows, other]
            out[par, :, rows] = jnp.swapaxes(sa, 0, 1)
            out[other, :, rows] = jnp.swapaxes(sb, 0, 1)
        else:
            out[rows, par] = sa
            out[rows, other] = sb


def in_vmem(value):
    return pltpu.with_memory_space_constraint(value, pltpu.VMEM)


def stencil(par, own, outer, inner, pot, base=None, token=None):
    combine = base is not None
    orbs, planes, ny, nz = own.shape
    args = (own, outer, inner, pot) + ((base, token) if combine else ())
    shape = (planes, ny, orbs, nz) if combine else own.shape
    return pl.pallas_call(
        lambda *refs: stencil_kernel(combine, *refs),
        out_shape=pltpu.VMEM(shape, own.dtype),
        in_specs=[pl.BlockSpec(memory_space=pltpu.SMEM)]
        + [pl.BlockSpec(memory_space=pltpu.VMEM)] * len(args),
        out_specs=pl.BlockSpec(memory_space=pltpu.VMEM),
        compiler_params=pltpu.CompilerParams(vmem_limit_bytes=4 << 20),
        name="stencil",
    )(par, *map(in_vmem, args))


def rotate_kernel(at_ref, v, *refs):
    pieces, out, wide = refs[:8], refs[8], refs[9]
    core, y = at_ref[0], at_ref[1]
    nx, nzl, rows, half = pieces[0].shape
    value = v[...]
    high = value.astype(jnp.bfloat16)
    low = (value - high.astype(jnp.float32)).astype(jnp.bfloat16)
    wide[...] = jnp.concatenate([high, low], axis=1)
    nz = v.shape[1]

    def product(piece, which):
        piece = piece[...].reshape(nx * nzl * rows, half)
        high = piece.astype(jnp.bfloat16)
        low = (piece - high.astype(jnp.float32)).astype(jnp.bfloat16)
        at = pl.ds(pl.multiple_of(which * half, half), half)
        both = jnp.dot(high, wide[at, :], preferred_element_type=jnp.float32)
        rest = jnp.dot(low, wide[at, :nz], preferred_element_type=jnp.float32)
        return both[:, :nz] + both[:, nz:] + rest

    for j, step in enumerate((0, 3, 1, 2)):
        total = product(pieces[2 * j], core) + product(pieces[2 * j + 1], 1 - core)
        place = pl.ds(pl.multiple_of(lax.rem(y + step, 4) * rows, rows), rows)
        for group in range(nx * nzl):
            out[group, place] = total[group * rows : (group + 1) * rows]


def rotate(at, v, pieces, shape):
    return pl.pallas_call(
        rotate_kernel,
        out_shape=pltpu.VMEM(shape, v.dtype),
        in_specs=[pl.BlockSpec(memory_space=pltpu.SMEM)]
        + [pl.BlockSpec(memory_space=pltpu.VMEM)] * (1 + len(pieces)),
        out_specs=pl.BlockSpec(memory_space=pltpu.VMEM),
        scratch_shapes=[pltpu.VMEM((v.shape[0], 2 * v.shape[1]), jnp.bfloat16)],
        compiler_params=pltpu.CompilerParams(vmem_limit_bytes=24 << 20),
        name="rotate",
    )(at, *map(in_vmem, (v, *pieces)))


def to_all(value, axis):
    copies = jnp.broadcast_to(value[None], (lax.axis_size(axis), *value.shape))
    return lax.all_to_all(copies, axis, 0, 0, tiled=True)


def gather_rotation(rot_t):
    ny = lax.axis_size("y")
    rows, cols = rot_t.shape[0] // 4, rot_t.shape[1] // 2
    at = ((lax.axis_index("y") % 4) * rows, lax.axis_index("c") * cols)
    up = [(i, (i + 1) % ny) for i in range(ny)]
    down = [(j, i) for i, j in up]
    part = to_all(lax.dynamic_slice(rot_t, at, (rows, cols)), "zl")
    own = to_all(part, "x")
    below = lax.ppermute(own, "y", up)
    above = lax.ppermute(own, "y", down)
    token = below[0, 0, :8, :128] * 2.0
    far = lax.ppermute(below, "y", up)
    pieces = []
    for piece in (own, below, above, far):
        pieces += [piece, lax.ppermute(piece, "c", [(0, 1), (1, 0)])]
    return pieces, token


def swap(value, pairs):
    return lax.ppermute(value, GRID, pairs)


def per_device(orbitals, potential, rotation):
    devices = lax.axis_size(GRID)
    outer_pairs = [(i, (i + 1 if i % 2 else i - 1) % devices) for i in range(devices)]
    inner_pairs = [(i, i ^ 1) for i in range(devices)]
    core = lax.axis_index("c")
    at = jnp.stack([core, lax.axis_index("y")]).astype(jnp.int32)
    pieces, token = gather_rotation(rotation.T)

    outer = swap(orbitals, outer_pairs)
    inner = swap(orbitals, inner_pairs)
    first = stencil(at, orbitals, outer, inner, potential)
    outer = swap(first, outer_pairs)
    inner = swap(first, inner_pairs)
    filtered = stencil(at, first, outer, inner, potential, orbitals, token)
    orbs, planes, ny, nz = orbitals.shape
    groups = lax.axis_size(BAND)
    parts = filtered.reshape(groups, -1, nz)
    parts = lax.all_to_all(parts, BAND, 0, 0, tiled=True)
    mixed = rotate(at, parts.reshape(groups * orbs, nz), pieces, (groups, orbs, nz))
    back = lax.all_to_all(mixed, BAND, 0, 0, tiled=True)
    return back.transpose(1, 0, 2).reshape(orbs, planes, ny, nz)


def run(fine):
    in_specs = (P(BAND, GRID, None, None), P(GRID, None, None), P(None, BAND))
    return jax.shard_map(
        per_device, mesh=fine, in_specs=in_specs, out_specs=P(BAND, GRID, None, None), check_vma=False
    )


def solution(mesh):
    devices = np.asarray(mesh.devices).reshape(8, 3, 2, 4, 4)
    fine = Mesh(devices, GRID + BAND)
    return run(fine)
```

```python
import jax
import jax.numpy as jnp
import numpy as np
from jax import lax
from jax.experimental import pallas as pl
from jax.experimental.pallas import tpu as pltpu
from jax.sharding import Mesh, PartitionSpec as P

GROUP = 8
LATE = (7,)
GRID = ("y", "zh", "c")
BAND = ("x", "zl")


def shifted_sums(c, axis):
    n = c.shape[axis]
    near = pltpu.roll(c, 1, axis) + pltpu.roll(c, n - 1, axis)
    far = pltpu.roll(c, 2, axis) + pltpu.roll(c, n - 2, axis)
    return near, far


def apply_plane(c, near_x, far_x, pot):
    near_y, far_y = shifted_sums(c, 1)
    near_z, far_z = shifted_sums(c, 2)
    near = near_x + near_y + near_z
    far = far_x + far_y + far_z
    return c * pot - (1.0 / 6.0) * near + (1.0 / 96.0) * far


def stencil_kernel(combine, par_ref, own, outer, inner, pot_ref, *rest):
    base, out = (rest[0], rest[-1]) if combine else (None, rest[0])
    par = par_ref[0]
    other = 1 - par
    pot_a = ((pot_ref[par] - 3.0) * 0.0625)[None]
    pot_b = ((pot_ref[other] - 3.0) * 0.0625)[None]

    @pl.loop(0, own.shape[0] // GROUP)
    def _(step):
        rows = pl.ds(step * GROUP, GROUP)
        a, b = own[rows, par], own[rows, other]
        o1, o2 = outer[rows, other], outer[rows, par]
        i1, i2 = inner[rows, par], inner[rows, other]
        sa = apply_plane(a, o1 + b, o2 + i1, pot_a)
        sb = apply_plane(b, a + i1, o1 + i2, pot_b)
        if combine:
            sa = 2.0 * sa - base[rows, par]
            sb = 2.0 * sb - base[rows, other]
            out[par, :, rows] = jnp.swapaxes(sa, 0, 1)
            out[other, :, rows] = jnp.swapaxes(sb, 0, 1)
        else:
            out[rows, par] = sa
            out[rows, other] = sb


def in_vmem(value):
    return pltpu.with_memory_space_constraint(value, pltpu.VMEM)


def stencil(par, own, outer, inner, pot, base=None, token=None):
    combine = base is not None
    orbs, planes, ny, nz = own.shape
    args = (own, outer, inner, pot) + ((base, token) if combine else ())
    shape = (planes, ny, orbs, nz) if combine else own.shape
    return pl.pallas_call(
        lambda *refs: stencil_kernel(combine, *refs),
        out_shape=pltpu.VMEM(shape, own.dtype),
        in_specs=[pl.BlockSpec(memory_space=pltpu.SMEM)]
        + [pl.BlockSpec(memory_space=pltpu.VMEM)] * len(args),
        out_specs=pl.BlockSpec(memory_space=pltpu.VMEM),
        compiler_params=pltpu.CompilerParams(vmem_limit_bytes=4 << 20),
        name="stencil",
    )(par, *map(in_vmem, args))


def rotate_kernel(at_ref, v, *refs):
    pieces, out, wide, landed, sems = list(refs[:8]), *refs[8:]
    copies = {}
    for slot, at in enumerate(LATE):
        copies[at] = pltpu.make_async_copy(pieces[at], landed.at[slot], sems.at[slot])
        copies[at].start()
        pieces[at] = landed.at[slot]
    core, y = at_ref[0], at_ref[1]
    nx, nzl, rows, half = pieces[0].shape
    value = v[...]
    high = value.astype(jnp.bfloat16)
    low = (value - high.astype(jnp.float32)).astype(jnp.bfloat16)
    wide[...] = jnp.concatenate([high, low], axis=1)
    nz = v.shape[1]

    def product(piece, which):
        piece = piece[...].reshape(nx * nzl * rows, half)
        high = piece.astype(jnp.bfloat16)
        low = (piece - high.astype(jnp.float32)).astype(jnp.bfloat16)
        at = pl.ds(pl.multiple_of(which * half, half), half)
        both = jnp.dot(high, wide[at, :], preferred_element_type=jnp.float32)
        rest = jnp.dot(low, wide[at, :nz], preferred_element_type=jnp.float32)
        return both[:, :nz] + both[:, nz:] + rest

    for j, step in enumerate((0, 3, 1, 2)):
        total = product(pieces[2 * j], core)
        if 2 * j + 1 in copies:
            copies[2 * j + 1].wait()
        total += product(pieces[2 * j + 1], 1 - core)
        place = pl.ds(pl.multiple_of(lax.rem(y + step, 4) * rows, rows), rows)
        for group in range(nx * nzl):
            out[group, place] = total[group * rows : (group + 1) * rows]


def rotate(at, v, pieces, shape):
    return pl.pallas_call(
        rotate_kernel,
        out_shape=pltpu.VMEM(shape, v.dtype),
        in_specs=[pl.BlockSpec(memory_space=pltpu.SMEM), pl.BlockSpec(memory_space=pltpu.VMEM)]
        + [pl.BlockSpec(memory_space=pltpu.HBM if at in LATE else pltpu.VMEM) for at in range(len(pieces))],
        out_specs=pl.BlockSpec(memory_space=pltpu.VMEM),
        scratch_shapes=[
            pltpu.VMEM((v.shape[0], 2 * v.shape[1]), jnp.bfloat16),
            pltpu.VMEM((len(LATE), *pieces[0].shape), jnp.float32),
            pltpu.SemaphoreType.DMA((len(LATE),)),
        ],
        compiler_params=pltpu.CompilerParams(vmem_limit_bytes=24 << 20),
        name="rotate",
    )(at, in_vmem(v), *(pltpu.with_memory_space_constraint(p, pltpu.HBM) if i in LATE else in_vmem(p) for i, p in enumerate(pieces)))


def pick_kernel(at_ref, source, out, sems):
    copies, rows, cols = out.shape
    at = (
        pl.ds(pl.multiple_of(lax.rem(at_ref[1], 4) * rows, rows), rows),
        pl.ds(pl.multiple_of(at_ref[0] * cols, cols), cols),
    )
    moves = [pltpu.make_async_copy(source.at[at], out.at[i], sems.at[i]) for i in range(copies)]
    for move in moves:
        move.start()
    for move in moves:
        move.wait()


def pick(at, source, shape):
    return pl.pallas_call(
        pick_kernel,
        out_shape=pltpu.VMEM(shape, source.dtype),
        in_specs=[pl.BlockSpec(memory_space=pltpu.SMEM), pl.BlockSpec(memory_space=pltpu.HBM)],
        out_specs=pl.BlockSpec(memory_space=pltpu.VMEM),
        scratch_shapes=[pltpu.SemaphoreType.DMA((shape[0],))],
        compiler_params=pltpu.CompilerParams(vmem_limit_bytes=1 << 20),
        name="pick",
    )(at, pltpu.with_memory_space_constraint(source, pltpu.HBM))


def to_all(value, axis):
    copies = jnp.broadcast_to(value[None], (lax.axis_size(axis), *value.shape))
    return lax.all_to_all(copies, axis, 0, 0, tiled=True)


def gather_rotation(at, rot_t):
    ny = lax.axis_size("y")
    rows, cols = rot_t.shape[0] // 4, rot_t.shape[1] // 2
    up = [(i, (i + 1) % ny) for i in range(ny)]
    down = [(j, i) for i, j in up]
    part = pick(at, rot_t, (lax.axis_size("zl"), rows, cols))
    part = lax.all_to_all(part, "zl", 0, 0, tiled=True)
    own = to_all(part, "x")
    below = lax.ppermute(own, "y", up)
    above = lax.ppermute(own, "y", down)
    token = below[0, 0, :8, :128] * 2.0
    far = lax.ppermute(below, "y", up)
    pieces = []
    for piece in (own, below, above, far):
        pieces += [piece, lax.ppermute(piece, "c", [(0, 1), (1, 0)])]
    return pieces, token


def swap(value, pairs):
    return lax.ppermute(value, GRID, pairs)


def per_device(orbitals, potential, rotation):
    devices = lax.axis_size(GRID)
    outer_pairs = [(i, (i + 1 if i % 2 else i - 1) % devices) for i in range(devices)]
    inner_pairs = [(i, i ^ 1) for i in range(devices)]
    core = lax.axis_index("c")
    at = jnp.stack([core, lax.axis_index("y")]).astype(jnp.int32)
    pieces, token = gather_rotation(at, rotation.T)

    outer = swap(orbitals, outer_pairs)
    inner = swap(orbitals, inner_pairs)
    first = stencil(at, orbitals, outer, inner, potential)
    outer = swap(first, outer_pairs)
    inner = swap(first, inner_pairs)
    filtered = stencil(at, first, outer, inner, potential, orbitals, token)
    orbs, planes, ny, nz = orbitals.shape
    groups = lax.axis_size(BAND)
    parts = filtered.reshape(groups, -1, nz)
    parts = lax.all_to_all(parts, BAND, 0, 0, tiled=True)
    mixed = rotate(at, parts.reshape(groups * orbs, nz), pieces, (groups, orbs, nz))
    back = lax.all_to_all(mixed, BAND, 0, 0, tiled=True)
    return back.transpose(1, 0, 2).reshape(orbs, planes, ny, nz)


def run(fine):
    in_specs = (P(BAND, GRID, None, None), P(GRID, None, None), P(None, BAND))
    return jax.shard_map(
        per_device, mesh=fine, in_specs=in_specs, out_specs=P(BAND, GRID, None, None), check_vma=False
    )


def solution(mesh):
    devices = np.asarray(mesh.devices).reshape(8, 3, 2, 4, 4)
    fine = Mesh(devices, GRID + BAND)
    return run(fine)
```

```python
import jax
import jax.numpy as jnp
import numpy as np
from jax import lax
from jax.experimental import pallas as pl
from jax.experimental.pallas import tpu as pltpu
from jax.sharding import Mesh, PartitionSpec as P

GROUP = 8
LATE = (1, 5, 7)
GRID = ("y", "zh", "c")
BAND = ("x", "zl")


def shifted_sums(c, axis):
    n = c.shape[axis]
    near = pltpu.roll(c, 1, axis) + pltpu.roll(c, n - 1, axis)
    far = pltpu.roll(c, 2, axis) + pltpu.roll(c, n - 2, axis)
    return near, far


def apply_plane(c, near_x, far_x, pot):
    near_y, far_y = shifted_sums(c, 1)
    near_z, far_z = shifted_sums(c, 2)
    near = near_x + near_y + near_z
    far = far_x + far_y + far_z
    return c * pot - (1.0 / 6.0) * near + (1.0 / 96.0) * far


def stencil_kernel(combine, par_ref, own, outer, inner, pot_ref, *rest):
    base, out = (rest[0], rest[-1]) if combine else (None, rest[0])
    par = par_ref[0]
    other = 1 - par
    pot_a = ((pot_ref[par] - 3.0) * 0.0625)[None]
    pot_b = ((pot_ref[other] - 3.0) * 0.0625)[None]

    @pl.loop(0, own.shape[0] // GROUP)
    def _(step):
        rows = pl.ds(step * GROUP, GROUP)
        a, b = own[rows, par], own[rows, other]
        o1, o2 = outer[rows, other], outer[rows, par]
        i1, i2 = inner[rows, par], inner[rows, other]
        sa = apply_plane(a, o1 + b, o2 + i1, pot_a)
        sb = apply_plane(b, a + i1, o1 + i2, pot_b)
        if combine:
            sa = 2.0 * sa - base[rows, par]
            sb = 2.0 * sb - base[rows, other]
            out[par, :, rows] = jnp.swapaxes(sa, 0, 1)
            out[other, :, rows] = jnp.swapaxes(sb, 0, 1)
        else:
            out[rows, par] = sa
            out[rows, other] = sb


def in_vmem(value):
    return pltpu.with_memory_space_constraint(value, pltpu.VMEM)


def stencil(par, own, outer, inner, pot, base=None, token=None):
    combine = base is not None
    orbs, planes, ny, nz = own.shape
    args = (own, outer, inner, pot) + ((base, token) if combine else ())
    shape = (planes, ny, orbs, nz) if combine else own.shape
    return pl.pallas_call(
        lambda *refs: stencil_kernel(combine, *refs),
        out_shape=pltpu.VMEM(shape, own.dtype),
        in_specs=[pl.BlockSpec(memory_space=pltpu.SMEM)]
        + [pl.BlockSpec(memory_space=pltpu.VMEM)] * len(args),
        out_specs=pl.BlockSpec(memory_space=pltpu.VMEM),
        compiler_params=pltpu.CompilerParams(vmem_limit_bytes=4 << 20),
        name="stencil",
    )(par, *map(in_vmem, args))


def rotate_kernel(at_ref, v, *refs):
    pieces, out, wide, landed, sems = list(refs[:8]), *refs[8:]
    copies = {}
    for slot, at in enumerate(LATE):
        copies[at] = pltpu.make_async_copy(pieces[at], landed.at[slot], sems.at[slot])
        copies[at].start()
        pieces[at] = landed.at[slot]
    core, y = at_ref[0], at_ref[1]
    nx, nzl, rows, half = pieces[0].shape
    value = v[...]
    high = value.astype(jnp.bfloat16)
    low = (value - high.astype(jnp.float32)).astype(jnp.bfloat16)
    wide[...] = jnp.concatenate([high, low], axis=1)
    nz = v.shape[1]

    def product(piece, which):
        piece = piece[...].reshape(nx * nzl * rows, half)
        high = piece.astype(jnp.bfloat16)
        low = (piece - high.astype(jnp.float32)).astype(jnp.bfloat16)
        at = pl.ds(pl.multiple_of(which * half, half), half)
        both = jnp.dot(high, wide[at, :], preferred_element_type=jnp.float32)
        rest = jnp.dot(low, wide[at, :nz], preferred_element_type=jnp.float32)
        return both[:, :nz] + both[:, nz:] + rest

    for j, step in ((1, 3), (0, 0), (2, 1), (3, 2)):
        total = product(pieces[2 * j], core)
        if 2 * j + 1 in copies:
            copies[2 * j + 1].wait()
        total += product(pieces[2 * j + 1], 1 - core)
        place = pl.ds(pl.multiple_of(lax.rem(y + step, 4) * rows, rows), rows)
        for group in range(nx * nzl):
            out[group, place] = total[group * rows : (group + 1) * rows]


def rotate(at, v, pieces, shape):
    return pl.pallas_call(
        rotate_kernel,
        out_shape=pltpu.VMEM(shape, v.dtype),
        in_specs=[pl.BlockSpec(memory_space=pltpu.SMEM), pl.BlockSpec(memory_space=pltpu.VMEM)]
        + [pl.BlockSpec(memory_space=pltpu.HBM if at in LATE else pltpu.VMEM) for at in range(len(pieces))],
        out_specs=pl.BlockSpec(memory_space=pltpu.VMEM),
        scratch_shapes=[
            pltpu.VMEM((v.shape[0], 2 * v.shape[1]), jnp.bfloat16),
            pltpu.VMEM((len(LATE), *pieces[0].shape), jnp.float32),
            pltpu.SemaphoreType.DMA((len(LATE),)),
        ],
        compiler_params=pltpu.CompilerParams(vmem_limit_bytes=24 << 20),
        name="rotate",
    )(at, in_vmem(v), *(pltpu.with_memory_space_constraint(p, pltpu.HBM) if i in LATE else in_vmem(p) for i, p in enumerate(pieces)))


def to_all(value, axis):
    copies = jnp.broadcast_to(value[None], (lax.axis_size(axis), *value.shape))
    return lax.all_to_all(copies, axis, 0, 0, tiled=True)


def gather_rotation(rot_t):
    ny = lax.axis_size("y")
    rows, cols = rot_t.shape[0] // 4, rot_t.shape[1] // 2
    at = ((lax.axis_index("y") % 4) * rows, lax.axis_index("c") * cols)
    up = [(i, (i + 1) % ny) for i in range(ny)]
    down = [(j, i) for i, j in up]
    part = to_all(lax.dynamic_slice(rot_t, at, (rows, cols)), "zl")
    own = to_all(part, "x")
    below = lax.ppermute(own, "y", up)
    above = lax.ppermute(own, "y", down)
    token = below[0, 0, :8, :128] * 2.0
    far = lax.ppermute(below, "y", up)
    pieces = []
    for piece in (own, below, above, far):
        pieces += [piece, lax.ppermute(piece, "c", [(0, 1), (1, 0)])]
    return pieces, token


def swap(value, pairs):
    return lax.ppermute(value, GRID, pairs)


def per_device(orbitals, potential, rotation):
    devices = lax.axis_size(GRID)
    outer_pairs = [(i, (i + 1 if i % 2 else i - 1) % devices) for i in range(devices)]
    inner_pairs = [(i, i ^ 1) for i in range(devices)]
    core = lax.axis_index("c")
    at = jnp.stack([core, lax.axis_index("y")]).astype(jnp.int32)
    pieces, token = gather_rotation(rotation.T)

    outer = swap(orbitals, outer_pairs)
    inner = swap(orbitals, inner_pairs)
    first = stencil(at, orbitals, outer, inner, potential)
    outer = swap(first, outer_pairs)
    inner = swap(first, inner_pairs)
    filtered = stencil(at, first, outer, inner, potential, orbitals, token)
    orbs, planes, ny, nz = orbitals.shape
    groups = lax.axis_size(BAND)
    parts = filtered.reshape(groups, -1, nz)
    parts = lax.all_to_all(parts, BAND, 0, 0, tiled=True)
    mixed = rotate(at, parts.reshape(groups * orbs, nz), pieces, (groups, orbs, nz))
    back = lax.all_to_all(mixed, BAND, 0, 0, tiled=True)
    return back.transpose(1, 0, 2).reshape(orbs, planes, ny, nz)


def run(fine):
    in_specs = (P(BAND, GRID, None, None), P(GRID, None, None), P(None, BAND))
    return jax.shard_map(
        per_device, mesh=fine, in_specs=in_specs, out_specs=P(BAND, GRID, None, None), check_vma=False
    )


def solution(mesh):
    devices = np.asarray(mesh.devices).reshape(8, 3, 2, 4, 4)
    fine = Mesh(devices, GRID + BAND)
    return run(fine)
```
